256 devices in a mesh: gx: 2 (over core), gy: 4 (over x), gz: 32 (over z, y).
Axes of the slice: x: 4, y: 4, z: 8, core: 2. Of those that a mesh axis runs over, the one named last changes fastest.
Arguments:
- a_blocks: bfloat16 [4, 8, 64, 64, 2048], P('gx', 'gy', 'gz'), may hold values from -0.15625 to 0.15625
- a_cols: int32 [4, 8, 64, 32], P('gx', 'gy', 'gz'), may hold values from 0 to 26, as said below
- a_count: int32 [4, 8, 64], P('gx', 'gy', 'gz'), may hold values from 14 to 27
- p_blocks: bfloat16 [4, 8, 64, 64, 512], P('gx', 'gy', 'gz'), may hold values from -0.75 to 0.75
- p_cols: int32 [4, 8, 64, 8], P('gx', 'gy', 'gz'), may hold values from 0 to 7, as said below
- p_count: int32 [4, 8, 64], P('gx', 'gy', 'gz'), may hold values from 1 to 8
- coarse_row: int32 [2, 4, 32], P('gx', 'gy', 'gz'), may hold values from 0 to 511, as said below
Outputs:
- coarse_matrix: bfloat16 [512, 64, 8192], P(('gx', 'gy', 'gz'))
The draws below stay inside these ranges and needn't reach their ends.
Inputs may be any that keep to these rules, and one draw needn't show every extreme that they name: `a_cols`: in each row the first a_count entries are distinct. `p_cols`: each row holds 0 to 7 once each, 0 in slot 0. `coarse_row`: values are distinct. Row r belongs to device r // 2 in mesh order; aggregate (u, v, w) goes to a row of a device with gx = u and gy = v. A device gets at most 2 aggregates, and in each group of devices with equal gx and gy one device gets exactly 2.
All inputs are finite; a program needn't handle non-finite values.
Results may differ from the reference program's by a relative error of at most 0.005.
Values may be sent and summed in bfloat16 or wider, within the bound.
No kernel may reach another device: no remote copies, remote signals or barrier semaphores. Data moves between devices by JAX's collectives and lax.ppermute only.
A program may use at most 192 MiB of HBM per device.

```python
import jax
import jax.numpy as jnp
from jax import lax

B = 64
K = 32
AZ = 1
NX = 4
NY = 8
NZ = 64
CAP = 2
ROWS = 512
N_GX = 2
N_GY = 4
N_GZ = 32


def draw_a_cols(key, part):
    row_count = NX * NY * NZ
    key_order, key_pad = jax.random.split(jax.random.fold_in(key, 11))
    scores = jax.random.randint(key_order, (row_count, 27), 0, 1 << 20) * 32 + jnp.arange(27)
    ordering = jnp.argsort(scores, axis=1).astype(jnp.int32)
    filler = jax.random.randint(key_pad, (row_count, K - 27), 0, 27).astype(jnp.int32)
    return jnp.concatenate([ordering, filler], axis=1).reshape(NX, NY, NZ, K).astype(jnp.int32)


def draw_p_cols(key, part):
    row_count = NX * NY * NZ
    scores = jax.random.randint(jax.random.fold_in(key, 13), (row_count, 7), 0, 1 << 20) * 8 + jnp.arange(7)
    ordering = jnp.argsort(scores, axis=1).astype(jnp.int32) + 1
    leading = jnp.zeros((row_count, 1), jnp.int32)
    return jnp.concatenate([leading, ordering], axis=1).reshape(NX, NY, NZ, 8).astype(jnp.int32)


def draw_coarse_row(key, part):
    group_count = N_GX * N_GY
    per_group = N_GZ * AZ

    def one_group(group_key, group_id):
        key_owner, key_order, key_other = jax.random.split(group_key, 3)
        busy_owner = jax.random.randint(key_owner, (), 0, N_GZ)
        ordering = jax.random.permutation(key_order, per_group)
        other_slots = jax.random.permutation(key_other, (N_GZ - 1) * CAP)[:per_group - CAP]
        other_slots = other_slots + CAP * (other_slots // CAP >= busy_owner).astype(jnp.int32)
        slot_list = jnp.concatenate([busy_owner * CAP + jnp.arange(CAP), other_slots]).astype(jnp.int32)
        chosen = jnp.zeros((per_group,), jnp.int32).at[ordering].set(slot_list)
        return group_id * N_GZ * CAP + chosen
    group_keys = jax.random.split(jax.random.fold_in(key, 29), group_count)
    result = jax.vmap(one_group)(group_keys, jnp.arange(group_count, dtype=jnp.int32))
    return result.reshape(N_GX, N_GY, per_group).astype(jnp.int32)


def plant(drawn, rng, low, largest):
    longest = drawn.shape.index(max(drawn.shape))
    spots = []
    for shift in (0, 1):
        where = [jax.random.randint(jax.random.fold_in(rng, axis), (), 0, length) for axis, length in enumerate(drawn.shape)]
        where[longest] = (where[longest] + shift) % drawn.shape[longest]
        spots.append(tuple(where))
    return drawn.at[spots[0]].set(low).at[spots[1]].set(largest)


def steps_of(rng, shape, cuts, least, high):
    def one(position, parts):
        steps = jax.random.uniform(jax.random.fold_in(jax.random.fold_in(rng, 6), position), (parts,), jnp.float32, least / len(cuts), high / len(cuts))
        return jnp.repeat(jnp.exp(steps), shape[position] // parts).reshape((-1,) + (1,) * (len(shape) - position - 1))

    gain = one(*cuts[0])
    for cut in cuts[1:]:
        gain = gain * one(*cut)
    return gain


def scatter_about(rng, shape, deviation, most, shards=(), kind=jnp.bfloat16):
    array = deviation * jax.random.normal(rng, shape, jnp.float32)
    if shards:
        array = array * steps_of(rng, shape, shards, -0.22, 0.18)
    return jnp.clip(array, -most, most).astype(kind)


def setup_inputs(seed: int = 0) -> dict:
    splits = jax.random.split(jax.random.key(seed), 8)
    a_blocks = scatter_about(splits[0], (NX, NY, NZ, B, K * B), (20 * B) ** -0.5, 0.15625, ((0, 2), (1, 4), (2, 32)))
    a_cols = draw_a_cols(jax.random.fold_in(splits[7], 71), 0)
    a_count = plant(jax.random.randint(splits[2], (NX, NY, NZ), 14, 28), jax.random.fold_in(splits[2], 1), 14, 27).astype(jnp.int32)
    p_blocks = scatter_about(splits[3], (NX, NY, NZ, B, 8 * B), B ** -0.5, 0.75, ((0, 2), (1, 4), (2, 32)))
    p_cols = draw_p_cols(jax.random.fold_in(splits[7], 71), 0)
    p_count = plant(jax.random.randint(splits[5], (NX, NY, NZ), 1, 9), jax.random.fold_in(splits[5], 1), 1, 8).astype(jnp.int32)
    coarse_row = draw_coarse_row(jax.random.fold_in(splits[7], 71), 0)
    return {"a_blocks": a_blocks, "a_cols": a_cols, "a_count": a_count, "p_blocks": p_blocks, "p_cols": p_cols, "p_count": p_count, "coarse_row": coarse_row}


CLASS_PICKS = ((0,), (1, 2), (3,))


def split_code(code_list):
    return code_list // 9 - 1, (code_list // 3) % 3 - 1, code_list % 3 - 1


def axis_slot(parity, offset, code_bit):
    landing = parity + offset
    shifted = jnp.floor_divide(landing, 2)
    facing = jnp.where(jnp.remainder(landing, 2) == 0, -1, 1)
    return shifted[:, None] + code_bit[None, :] * facing[:, None]


def slot_table(parity_x, parity_y, parity_z, code_list, live_count):
    offset_x, offset_y, offset_z = split_code(code_list)
    code_range = jnp.arange(8, dtype=jnp.int32)
    slot_x = axis_slot(parity_x, offset_x, code_range % 2)
    slot_y = axis_slot(parity_y, offset_y, (code_range // 2) % 2)
    slot_z = axis_slot(parity_z, offset_z, code_range // 4)
    target = (slot_x + 1) * 9 + (slot_y + 1) * 3 + (slot_z + 1)
    live = jnp.arange(code_list.shape[0], dtype=jnp.int32) < live_count
    return (target[:, :, None] == jnp.arange(28, dtype=jnp.int32)[None, None, :]) & live[:, None, None]


def place_rows(p_blocks, p_cols, p_count):
    shape_in = p_blocks.shape
    block_size = shape_in[3]
    blocks = p_blocks.astype(jnp.float32).reshape(shape_in[:3] + (block_size, 8, block_size))
    code_range = jnp.arange(8, dtype=jnp.int32)
    live = code_range < p_count[..., None]
    chooser = ((p_cols[..., None] == code_range) & live[..., None]).astype(jnp.float32)
    placed = jnp.einsum("xyzqc,xyzfqb->xyzfcb", chooser, blocks)
    return placed.astype(jnp.bfloat16).reshape(shape_in)


def coarse_sum(wide_placed, wide_product, block_size):
    extent = wide_product.shape[:3]
    groups = tuple((size_along - 2) // 2 for size_along in extent)
    total = jnp.zeros(groups + (block_size, 5, 5, 5, block_size), jnp.float32)
    for class_x in range(3):
        for class_y in range(3):
            for class_z in range(3):
                code = (class_x != 1) * 1 + (class_y != 1) * 2 + (class_z != 1) * 4
                partial_value = jnp.zeros(groups + (block_size, 28 * block_size), jnp.float32)
                for start_x in CLASS_PICKS[class_x]:
                    for start_y in CLASS_PICKS[class_y]:
                        for start_z in CLASS_PICKS[class_z]:
                            window = (slice(start_x, start_x + 2 * groups[0] - 1, 2),
                                      slice(start_y, start_y + 2 * groups[1] - 1, 2),
                                      slice(start_z, start_z + 2 * groups[2] - 1, 2))
                            blocks_p = wide_placed[window][..., code * block_size:(code + 1) * block_size].astype(jnp.float32)
                            blocks_ap = wide_product[window].astype(jnp.float32)
                            partial_value = partial_value + jnp.einsum("uvwfa,uvwfe->uvwae", blocks_p, blocks_ap)
                partial_value = partial_value.reshape(groups + (block_size, 28, block_size))[..., :27, :]
                partial_value = partial_value.reshape(groups + (block_size, 3, 3, 3, block_size))
                total = total.at[:, :, :, :, class_x:class_x + 3, class_y:class_y + 3, class_z:class_z + 3, :].add(partial_value)
    return total


def reference(a_blocks, a_cols, a_count, p_blocks, p_cols, p_count, coarse_row):
    placed = place_rows(p_blocks, p_cols, p_count)
    padded = jnp.pad(placed, ((1, 1), (1, 1), (1, 1), (0, 0), (0, 0)))
    flat_placed = padded.reshape(-1, B, 8 * B)
    total_rows = NX * NY * NZ
    row_ids = jnp.arange(total_rows, dtype=jnp.int32)
    coord_x = row_ids // (NY * NZ)
    coord_y = (row_ids // NZ) % NY
    coord_z = row_ids % NZ

    def one_row(row_item):
        row_blocks, code_list, live_count, at_x, at_y, at_z = row_item
        offset_x, offset_y, offset_z = split_code(code_list)
        flat_index = ((at_x + offset_x + 1) * (NY + 2) + (at_y + offset_y + 1)) * (NZ + 2) + (at_z + offset_z + 1)
        pieces = jnp.take(flat_placed, flat_index.astype(jnp.int32), axis=0).astype(jnp.float32).reshape(K, B, 8, B)
        chooser = slot_table(at_x % 2, at_y % 2, at_z % 2, code_list, live_count).astype(jnp.float32)
        a_row = row_blocks.astype(jnp.float32).reshape(B, K, B)
        partial_value = jnp.einsum("akc,kcqb->kaqb", a_row, pieces)
        summed = jnp.einsum("kqe,kaqb->aeb", chooser, partial_value, precision=lax.Precision.HIGHEST)
        return summed.reshape(B, 28 * B).astype(jnp.bfloat16)

    product = lax.map(one_row, (a_blocks.reshape(total_rows, B, K * B), a_cols.reshape(total_rows, K),
                                a_count.reshape(total_rows), coord_x, coord_y, coord_z))
    product = product.reshape(NX, NY, NZ, B, 28 * B)
    wide_product = jnp.pad(product, ((1, 1), (1, 1), (1, 1), (0, 0), (0, 0)))
    total = coarse_sum(padded, wide_product, B)
    coarse_rows = total.reshape(-1, B, 125 * B)
    coarse_rows = jnp.pad(coarse_rows, ((0, 0), (0, 0), (0, 3 * B))).astype(jnp.bfloat16)
    result = jnp.zeros((ROWS, B, 128 * B), jnp.bfloat16)
    return result.at[coarse_row.reshape(-1).astype(jnp.int32)].set(coarse_rows)
```

```python
import jax
import jax.numpy as jnp
import numpy as np
from jax import lax
from jax.experimental import pallas as pl
from jax.experimental.pallas import tpu as pltpu
from jax.sharding import PartitionSpec as P

B = 64
REACH = (((-1, 0), (1,)), ((-1,), (0, 1)))
NAMED_BY = (((0, 0),), ((0, 1), (1, 0)), ((1, 1),))


def ring(axis):
    peers = lax.axis_size(axis)
    up = [(i, i + 1) for i in range(peers - 1)]
    return up, [(j, i) for i, j in up]


def extend(shard):
    for dim, axis in enumerate(("gx", "gy", "gz")):
        up, down = ring(axis)
        length = shard.shape[dim]
        before = lax.ppermute(lax.slice_in_dim(shard, length - 1, length, axis=dim), axis, up)
        after = lax.ppermute(lax.slice_in_dim(shard, 0, 1, axis=dim), axis, down)
        shard = jnp.concatenate([before, shard, after], axis=dim)
    return shard


def place_rows(p_blocks, p_cols, p_count):
    code_of = np.zeros((8, 8), np.int32)
    for row in range(8):
        parity = (row >> 2, (row >> 1) & 1, row & 1)
        for pos in range(8):
            bits = (pos >> 2, (pos >> 1) & 1, pos & 1)
            code_of[row, pos] = sum((b if s else 1 - b) << d for d, (b, s) in enumerate(zip(bits, parity)))
    blocks = p_blocks.reshape(8, B, 8 * B)
    slots = jnp.arange(8, dtype=jnp.int32)
    code = jnp.where(slots < p_count.reshape(8, 1), p_cols.reshape(8, 8), -1)
    code = jnp.repeat(code, B, axis=1)
    wanted = jnp.repeat(jnp.asarray(code_of), B, axis=1)
    lane = jnp.arange(8 * B, dtype=jnp.int32) % B
    pick = (code[:, :, None] == wanted[:, None, :]) & (lane[:, None] == lane[None, :])[None]
    placed = jnp.einsum(
        "rfk,rks->rfs", blocks, pick.astype(jnp.bfloat16), preferred_element_type=jnp.float32
    )
    return placed.astype(jnp.bfloat16).reshape(2, 2, 2, B, 8 * B)


def wide_index(x, y, z):
    return (x + 1) * 16 + (y + 1) * 4 + (z + 1)


def galerkin_kernel(cols, count, a_ref, wide_ref, low_ref, mid_ref, high_ref, slot_ref, left_ref, prod_ref):
    left_ref[...] = jnp.zeros(left_ref.shape, left_ref.dtype)
    for row in range(8):
        parity = (row >> 2, (row >> 1) & 1, row & 1)
        slot_ref[...] = jnp.zeros(slot_ref.shape, slot_ref.dtype)
        for k in range(27):
            at = jnp.where(k < count[row], cols[row, k], 27)
            slot_ref[at] = a_ref[row, :, k * B : (k + 1) * B]
        slabs = {}
        for gx in range(2):
            for gy in range(2):
                for gz in range(2):
                    near = [
                        (ox, oy, oz)
                        for ox in REACH[parity[0]][gx]
                        for oy in REACH[parity[1]][gy]
                        for oz in REACH[parity[2]][gz]
                    ]
                    a_side = jnp.concatenate(
                        [slot_ref[(ox + 1) * 9 + (oy + 1) * 3 + oz + 1] for ox, oy, oz in near], axis=1
                    )
                    p_side = jnp.concatenate(
                        [
                            wide_ref[wide_index(parity[0] + ox, parity[1] + oy, parity[2] + oz)]
                            for ox, oy, oz in near
                        ],
                        axis=0,
                    )
                    cube = jnp.dot(a_side, p_side, preferred_element_type=jnp.float32)
                    for px in range(2):
                        for py in range(2):
                            key = (gx + px, gy + py, gz)
                            piece = cube[:, (px * 2 + py) * 128 : (px * 2 + py + 1) * 128]
                            slabs[key] = slabs[key] + piece if key in slabs else piece
        gap = jnp.zeros((B, B), jnp.float32)
        for e0 in range(3):
            for e1 in range(3):
                slab = jnp.concatenate([slabs[e0, e1, 0], gap], axis=1) + jnp.concatenate(
                    [gap, slabs[e0, e1, 1]], axis=1
                )
                prod_ref[e0 * 3 + e1, row * B : (row + 1) * B, :] = slab.astype(jnp.bfloat16)
        turned = wide_ref[wide_index(*parity)].T
        for dx in range(3):
            for dy in range(3):
                for dz in range(3):
                    pos = 0
                    for d, s in zip((dx, dy, dz), parity):
                        hit = [p for q, p in NAMED_BY[d] if q == s]
                        pos = pos * 2 + hit[0] if hit and pos is not None else None
                        if pos is None:
                            break
                    if pos is None:
                        continue
                    first = (dz * 9 + dy * 3 + dx) * B
                    left_ref[first : first + B, row * B : (row + 1) * B] = turned[pos * B : (pos + 1) * B, :]
    for dz, out_ref in enumerate((low_ref, mid_ref, high_ref)):
        left = left_ref[dz * 9 * B : (dz + 1) * 9 * B, :]
        for m in range(9):
            part = jnp.dot(left, prod_ref[m], preferred_element_type=jnp.float32)
            out_ref[:, m] = part.astype(out_ref.dtype).reshape(9, B, 3 * B)


def contributions(a_blocks, a_cols, a_count, wide_placed, interpret=False):
    smem = pl.BlockSpec(memory_space=pltpu.SMEM)
    vmem = pl.BlockSpec(memory_space=pltpu.VMEM)
    return pl.pallas_call(
        galerkin_kernel,
        out_shape=[
            jax.ShapeDtypeStruct((9, 9, B, 3 * B), kind)
            for kind in (jnp.bfloat16, jnp.float32, jnp.bfloat16)
        ],
        in_specs=[smem, smem, vmem, vmem],
        out_specs=[vmem] * 3,
        scratch_shapes=[
            pltpu.VMEM((28, B, B), jnp.bfloat16),
            pltpu.VMEM((27 * B, 8 * B), jnp.bfloat16),
            pltpu.VMEM((9, 8 * B, 3 * B), jnp.bfloat16),
        ],
        interpret=interpret,
    )(a_cols.reshape(8, -1), a_count.reshape(8), a_blocks.reshape(8, B, -1), wide_placed.reshape(64, B, 8 * B))


def fold(low, mid, high, axis, dim, width):
    up, down = ring(axis)
    from_below = lax.ppermute(high.astype(jnp.bfloat16), axis, up)
    from_above = lax.ppermute(low.astype(jnp.bfloat16), axis, down)

    def spread(part, before, after):
        pads = [(0, 0, 0)] * part.ndim
        pads[dim] = (before * width, after * width, 0)
        return lax.pad(part.astype(jnp.float32), jnp.float32(0), pads)

    return spread(from_below, 0, 2) + spread(mid, 1, 1) + spread(from_above, 2, 0)


def local(a_blocks, a_cols, a_count, p_blocks, p_cols, p_count, coarse_row, interpret=False):
    group_size = lax.axis_size("gz")
    target = jnp.broadcast_to(coarse_row.reshape(1, 1), (group_size, 1))
    targets = lax.all_to_all(target, "gz", split_axis=0, concat_axis=0, tiled=True).reshape(group_size)

    wide_placed = extend(place_rows(p_blocks, p_cols, p_count))
    low, mid, high = contributions(a_blocks, a_cols, a_count, wide_placed, interpret)
    part = fold(low, mid, high, "gz", 3, B).reshape(3, 3, 3, 3, B, 5 * B)
    part = fold(part[0], part[1], part[2], "gy", 2, 1)
    part = fold(part[0], part[1], part[2], "gx", 0, 1).astype(jnp.bfloat16)
    coarse = part.reshape(25, B, 5 * B).transpose(1, 0, 2).reshape(B, 125 * B)
    coarse = jnp.pad(coarse, ((0, 0), (0, 3 * B)))

    width = 128 * B // group_size
    spread = coarse.reshape(B, group_size, width).transpose(1, 0, 2)
    pieces = lax.all_to_all(spread, "gz", split_axis=0, concat_axis=0, tiled=True)
    group = lax.axis_index("gx") * lax.axis_size("gy") + lax.axis_index("gy")
    slots = group * (2 * group_size) + jnp.arange(2 * group_size, dtype=jnp.int32)
    matches = slots[:, None] == targets[None, :]
    source = jnp.argmax(matches, axis=1).astype(jnp.int32)
    taken = jnp.any(matches, axis=1)
    sent = jnp.take(pieces, source, axis=0, mode="clip")
    sent = jnp.where(taken[:, None, None], sent, jnp.zeros((), jnp.bfloat16))
    mine = lax.all_to_all(sent, "gz", split_axis=0, concat_axis=0, tiled=True)
    return mine.reshape(group_size, 2, B, width).transpose(1, 2, 0, 3).reshape(2, B, 128 * B)


def solution(mesh):
    in_specs = (
        P("gx", "gy", "gz", None, None),
        P("gx", "gy", "gz", None),
        P("gx", "gy", "gz"),
        P("gx", "gy", "gz", None, None),
        P("gx", "gy", "gz", None),
        P("gx", "gy", "gz"),
        P("gx", "gy", "gz"),
    )
    out_specs = P(("gx", "gy", "gz"), None, None)
    return jax.shard_map(local, mesh=mesh, in_specs=in_specs, out_specs=out_specs, check_vma=False)
```

```python
import jax
import jax.numpy as jnp
import numpy as np
from jax import lax
from jax.experimental import pallas as pl
from jax.experimental.pallas import tpu as pltpu
from jax.sharding import PartitionSpec as P

B = 64
REACH = (((-1, 0), (1,)), ((-1,), (0, 1)))
NAMED_BY = (((0, 0),), ((0, 1), (1, 0)), ((1, 1),))


def ring(axis):
    peers = lax.axis_size(axis)
    up = [(i, i + 1) for i in range(peers - 1)]
    return up, [(j, i) for i, j in up]


def extend(shard):
    for dim, axis in ((2, "gz"), (1, "gy"), (0, "gx")):
        up, down = ring(axis)
        length = shard.shape[dim]
        before = lax.ppermute(lax.slice_in_dim(shard, length - 1, length, axis=dim), axis, up)
        after = lax.ppermute(lax.slice_in_dim(shard, 0, 1, axis=dim), axis, down)
        shard = jnp.concatenate([before, shard, after], axis=dim)
    return shard


def place_rows(p_blocks, p_cols, p_count):
    code_of = np.zeros((8, 8), np.int32)
    for row in range(8):
        parity = (row >> 2, (row >> 1) & 1, row & 1)
        for pos in range(8):
            bits = (pos >> 2, (pos >> 1) & 1, pos & 1)
            code_of[row, pos] = sum((b if s else 1 - b) << d for d, (b, s) in enumerate(zip(bits, parity)))
    blocks = p_blocks.reshape(8, B, 8 * B)
    slots = jnp.arange(8, dtype=jnp.int32)
    code = jnp.where(slots < p_count.reshape(8, 1), p_cols.reshape(8, 8), -1)
    code = jnp.repeat(code, B, axis=1)
    wanted = jnp.repeat(jnp.asarray(code_of), B, axis=1)
    lane = jnp.arange(8 * B, dtype=jnp.int32) % B
    pick = (code[:, :, None] == wanted[:, None, :]) & (lane[:, None] == lane[None, :])[None]
    placed = jnp.einsum(
        "rfk,rks->rfs", blocks, pick.astype(jnp.bfloat16), preferred_element_type=jnp.float32
    )
    return placed.astype(jnp.bfloat16).reshape(2, 2, 2, B, 8 * B)


def wide_index(x, y, z):
    return (x + 1) * 16 + (y + 1) * 4 + (z + 1)


def galerkin_kernel(cols, count, a_ref, wide_ref, low_ref, mid_ref, high_ref, slot_ref, left_ref, prod_ref):
    left_ref[...] = jnp.zeros(left_ref.shape, left_ref.dtype)
    for row in range(8):
        parity = (row >> 2, (row >> 1) & 1, row & 1)
        slot_ref[...] = jnp.zeros(slot_ref.shape, slot_ref.dtype)
        for k in range(27):
            at = jnp.where(k < count[row], cols[row, k], 27)
            slot_ref[at] = a_ref[row, :, k * B : (k + 1) * B]
        slabs = {}
        for gx in range(2):
            for gy in range(2):
                for gz in range(2):
                    near = [
                        (ox, oy, oz)
                        for ox in REACH[parity[0]][gx]
                        for oy in REACH[parity[1]][gy]
                        for oz in REACH[parity[2]][gz]
                    ]
                    a_side = jnp.concatenate(
                        [slot_ref[(ox + 1) * 9 + (oy + 1) * 3 + oz + 1] for ox, oy, oz in near], axis=1
                    )
                    p_side = jnp.concatenate(
                        [
                            wide_ref[wide_index(parity[0] + ox, parity[1] + oy, parity[2] + oz)]
                            for ox, oy, oz in near
                        ],
                        axis=0,
                    )
                    cube = jnp.dot(a_side, p_side, preferred_element_type=jnp.float32)
                    for px in range(2):
                        for py in range(2):
                            key = (gx + px, gy + py, gz)
                            piece = cube[:, (px * 2 + py) * 128 : (px * 2 + py + 1) * 128]
                            slabs[key] = slabs[key] + piece if key in slabs else piece
        gap = jnp.zeros((B, B), jnp.float32)
        for e0 in range(3):
            for e1 in range(3):
                slab = jnp.concatenate([slabs[e0, e1, 0], gap], axis=1) + jnp.concatenate(
                    [gap, slabs[e0, e1, 1]], axis=1
                )
                prod_ref[e0 * 3 + e1, row * B : (row + 1) * B, :] = slab.astype(jnp.bfloat16)
        turned = wide_ref[wide_index(*parity)].T
        for dx in range(3):
            for dy in range(3):
                for dz in range(3):
                    pos = 0
                    for d, s in zip((dx, dy, dz), parity):
                        hit = [p for q, p in NAMED_BY[d] if q == s]
                        pos = pos * 2 + hit[0] if hit and pos is not None else None
                        if pos is None:
                            break
                    if pos is None:
                        continue
                    first = (dx * 9 + dz * 3 + dy) * B
                    left_ref[first : first + B, row * B : (row + 1) * B] = turned[pos * B : (pos + 1) * B, :]
    for dx, out_ref in enumerate((low_ref, mid_ref, high_ref)):
        left = left_ref[dx * 9 * B : (dx + 1) * 9 * B, :]
        for m in range(9):
            part = jnp.dot(left, prod_ref[m], preferred_element_type=jnp.float32)
            out_ref[:, m] = part.astype(out_ref.dtype).reshape(9, B, 3 * B)


def contributions(a_blocks, a_cols, a_count, wide_placed, interpret=False):
    smem = pl.BlockSpec(memory_space=pltpu.SMEM)
    vmem = pl.BlockSpec(memory_space=pltpu.VMEM)
    return pl.pallas_call(
        galerkin_kernel,
        out_shape=[
            jax.ShapeDtypeStruct((9, 9, B, 3 * B), kind)
            for kind in (jnp.bfloat16, jnp.float32, jnp.bfloat16)
        ],
        in_specs=[smem, smem, vmem, vmem],
        out_specs=[vmem] * 3,
        scratch_shapes=[
            pltpu.VMEM((28, B, B), jnp.bfloat16),
            pltpu.VMEM((27 * B, 8 * B), jnp.bfloat16),
            pltpu.VMEM((9, 8 * B, 3 * B), jnp.bfloat16),
        ],
        interpret=interpret,
    )(a_cols.reshape(8, -1), a_count.reshape(8), a_blocks.reshape(8, B, -1), wide_placed.reshape(64, B, 8 * B))


def fold(low, mid, high, axis, dim, width):
    up, down = ring(axis)
    from_below = lax.ppermute(high.astype(jnp.bfloat16), axis, up)
    from_above = lax.ppermute(low.astype(jnp.bfloat16), axis, down)

    def spread(part, before, after):
        pads = [(0, 0, 0)] * part.ndim
        pads[dim] = (before * width, after * width, 0)
        return lax.pad(part.astype(jnp.float32), jnp.float32(0), pads)

    return spread(from_below, 0, 2) + spread(mid, 1, 1) + spread(from_above, 2, 0)


def local(a_blocks, a_cols, a_count, p_blocks, p_cols, p_count, coarse_row, interpret=False):
    group_size = lax.axis_size("gz")
    target = jnp.broadcast_to(coarse_row.reshape(1, 1), (group_size, 1))
    targets = lax.all_to_all(target, "gz", split_axis=0, concat_axis=0, tiled=True).reshape(group_size)

    wide_placed = extend(place_rows(p_blocks, p_cols, p_count))
    wide_placed, targets = lax.optimization_barrier((wide_placed, targets))
    low, mid, high = contributions(a_blocks, a_cols, a_count, wide_placed, interpret)
    low, mid, high = (x.reshape(9, 3, 3, B, 3 * B) for x in (low, mid, high))
    part = fold(low, mid, high, "gx", 1, 1).reshape(3, 3, 5, 3, B, 3 * B)
    part = fold(part[0], part[1], part[2], "gz", 4, B)
    part = fold(part[0], part[1], part[2], "gy", 1, 1).astype(jnp.bfloat16)
    coarse = part.reshape(25, B, 5 * B).transpose(1, 0, 2).reshape(B, 125 * B)
    coarse = jnp.pad(coarse, ((0, 0), (0, 3 * B)))

    width = 128 * B // group_size
    spread = coarse.reshape(B, group_size, width).transpose(1, 0, 2)
    pieces = lax.all_to_all(spread, "gz", split_axis=0, concat_axis=0, tiled=True)
    group = lax.axis_index("gx") * lax.axis_size("gy") + lax.axis_index("gy")
    slots = group * (2 * group_size) + jnp.arange(2 * group_size, dtype=jnp.int32)
    matches = slots[:, None] == targets[None, :]
    source = jnp.argmax(matches, axis=1).astype(jnp.int32)
    taken = jnp.any(matches, axis=1)
    sent = jnp.take(pieces, source, axis=0, mode="clip")
    sent = jnp.where(taken[:, None, None], sent, jnp.zeros((), jnp.bfloat16))
    mine = lax.all_to_all(sent, "gz", split_axis=0, concat_axis=0, tiled=True)
    return mine.reshape(group_size, 2, B, width).transpose(1, 2, 0, 3).reshape(2, B, 128 * B)


def solution(mesh):
    in_specs = (
        P("gx", "gy", "gz", None, None),
        P("gx", "gy", "gz", None),
        P("gx", "gy", "gz"),
        P("gx", "gy", "gz", None, None),
        P("gx", "gy", "gz", None),
        P("gx", "gy", "gz"),
        P("gx", "gy", "gz"),
    )
    out_specs = P(("gx", "gy", "gz"), None, None)
    return jax.shard_map(local, mesh=mesh, in_specs=in_specs, out_specs=out_specs, check_vma=False)
```

```python
import jax
import jax.numpy as jnp
import numpy as np
from jax import lax
from jax.experimental import pallas as pl
from jax.experimental.pallas import tpu as pltpu
from jax.sharding import PartitionSpec as P

B = 64
REACH = (((-1, 0), (1,)), ((-1,), (0, 1)))
NAMED_BY = (((0, 0),), ((0, 1), (1, 0)), ((1, 1),))


def ring(axis):
    peers = lax.axis_size(axis)
    up = [(i, i + 1) for i in range(peers - 1)]
    return up, [(j, i) for i, j in up]


def extend(shard):
    for dim, axis in ((2, "gz"), (1, "gy"), (0, "gx")):
        up, down = ring(axis)
        length = shard.shape[dim]
        before = lax.ppermute(lax.slice_in_dim(shard, length - 1, length, axis=dim), axis, up)
        after = lax.ppermute(lax.slice_in_dim(shard, 0, 1, axis=dim), axis, down)
        shard = jnp.concatenate([before, shard, after], axis=dim)
    return shard


def place_rows(p_blocks, p_cols, p_count):
    code_of = np.zeros((8, 8), np.int32)
    for row in range(8):
        parity = (row >> 2, (row >> 1) & 1, row & 1)
        for pos in range(8):
            bits = (pos >> 2, (pos >> 1) & 1, pos & 1)
            code_of[row, pos] = sum((b if s else 1 - b) << d for d, (b, s) in enumerate(zip(bits, parity)))
    blocks = p_blocks.reshape(8, B, 8 * B)
    slots = jnp.arange(8, dtype=jnp.int32)
    code = jnp.where(slots < p_count.reshape(8, 1), p_cols.reshape(8, 8), -1)
    code = jnp.repeat(code, B, axis=1)
    wanted = jnp.repeat(jnp.asarray(code_of), B, axis=1)
    lane = jnp.arange(8 * B, dtype=jnp.int32) % B
    pick = (code[:, :, None] == wanted[:, None, :]) & (lane[:, None] == lane[None, :])[None]
    placed = jnp.einsum(
        "rfk,rks->rfs", blocks, pick.astype(jnp.bfloat16), preferred_element_type=jnp.float32
    )
    return placed.astype(jnp.bfloat16).reshape(2, 2, 2, B, 8 * B)


def wide_index(x, y, z):
    return (x + 1) * 16 + (y + 1) * 4 + (z + 1)


def galerkin_kernel(cols, count, a_ref, wide_ref, low_ref, mid_ref, high_ref, slot_ref, left_ref, prod_ref):
    left_ref[...] = jnp.zeros(left_ref.shape, left_ref.dtype)
    for row in range(8):
        parity = (row >> 2, (row >> 1) & 1, row & 1)
        slot_ref[...] = jnp.zeros(slot_ref.shape, slot_ref.dtype)
        for k in range(27):
            at = jnp.where(k < count[row], cols[row, k], 27)
            slot_ref[at] = a_ref[row, :, k * B : (k + 1) * B]
        slabs = {}
        for gx in range(2):
            for gy in range(2):
                for gz in range(2):
                    near = [
                        (ox, oy, oz)
                        for ox in REACH[parity[0]][gx]
                        for oy in REACH[parity[1]][gy]
                        for oz in REACH[parity[2]][gz]
                    ]
                    a_side = jnp.concatenate(
                        [slot_ref[(ox + 1) * 9 + (oy + 1) * 3 + oz + 1] for ox, oy, oz in near], axis=1
                    )
                    p_side = jnp.concatenate(
                        [
                            wide_ref[wide_index(parity[0] + ox, parity[1] + oy, parity[2] + oz)]
                            for ox, oy, oz in near
                        ],
                        axis=0,
                    )
                    cube = jnp.dot(a_side, p_side, preferred_element_type=jnp.float32)
                    for px in range(2):
                        for py in range(2):
                            key = (gx + px, gy + py, gz)
                            piece = cube[:, (px * 2 + py) * 128 : (px * 2 + py + 1) * 128]
                            slabs[key] = slabs[key] + piece if key in slabs else piece
        gap = jnp.zeros((B, B), jnp.float32)
        for e0 in range(3):
            for e1 in range(3):
                slab = jnp.concatenate([slabs[e0, e1, 0], gap], axis=1) + jnp.concatenate(
                    [gap, slabs[e0, e1, 1]], axis=1
                )
                prod_ref[e0 * 3 + e1, row * B : (row + 1) * B, :] = slab.astype(jnp.bfloat16)
        turned = wide_ref[wide_index(*parity)].T
        for dx in range(3):
            for dy in range(3):
                for dz in range(3):
                    pos = 0
                    for d, s in zip((dx, dy, dz), parity):
                        hit = [p for q, p in NAMED_BY[d] if q == s]
                        pos = pos * 2 + hit[0] if hit and pos is not None else None
                        if pos is None:
                            break
                    if pos is None:
                        continue
                    first = (dx * 9 + dz * 3 + dy) * B
                    left_ref[first : first + B, row * B : (row + 1) * B] = turned[pos * B : (pos + 1) * B, :]
    for dx, out_ref in enumerate((low_ref, mid_ref, high_ref)):
        left = left_ref[dx * 9 * B : (dx + 1) * 9 * B, :]
        for m in range(9):
            part = jnp.dot(left, prod_ref[m], preferred_element_type=jnp.float32)
            out_ref[:, m] = part.astype(out_ref.dtype).reshape(9, B, 3 * B)


def contributions(a_blocks, a_cols, a_count, wide_placed, interpret=False):
    smem = pl.BlockSpec(memory_space=pltpu.SMEM)
    vmem = pl.BlockSpec(memory_space=pltpu.VMEM)
    return pl.pallas_call(
        galerkin_kernel,
        out_shape=[
            jax.ShapeDtypeStruct((9, 9, B, 3 * B), kind)
            for kind in (jnp.bfloat16, jnp.float32, jnp.bfloat16)
        ],
        in_specs=[smem, smem, vmem, vmem],
        out_specs=[vmem] * 3,
        scratch_shapes=[
            pltpu.VMEM((28, B, B), jnp.bfloat16),
            pltpu.VMEM((27 * B, 8 * B), jnp.bfloat16),
            pltpu.VMEM((9, 8 * B, 3 * B), jnp.bfloat16),
        ],
        interpret=interpret,
    )(a_cols.reshape(8, -1), a_count.reshape(8), a_blocks.reshape(8, B, -1), wide_placed.reshape(64, B, 8 * B))


def fold(low, mid, high, axis, dim, width):
    up, down = ring(axis)
    from_below = lax.ppermute(high.astype(jnp.bfloat16), axis, up)
    from_above = lax.ppermute(low.astype(jnp.bfloat16), axis, down)

    def spread(part, before, after):
        pads = [(0, 0, 0)] * part.ndim
        pads[dim] = (before * width, after * width, 0)
        return lax.pad(part.astype(jnp.float32), jnp.float32(0), pads)

    return spread(from_below, 0, 2) + spread(mid, 1, 1) + spread(from_above, 2, 0)


def local(a_blocks, a_cols, a_count, p_blocks, p_cols, p_count, coarse_row, interpret=False):
    group_size = lax.axis_size("gz")
    target = jnp.broadcast_to(coarse_row.reshape(1, 1), (group_size, 1))
    targets = lax.all_to_all(target, "gz", split_axis=0, concat_axis=0, tiled=True).reshape(group_size)

    wide_placed = extend(place_rows(p_blocks, p_cols, p_count))
    low, mid, high = contributions(a_blocks, a_cols, a_count, wide_placed, interpret)
    low, mid, high = (x.reshape(9, 3, 3, B, 3 * B) for x in (low, mid, high))
    part = fold(low, mid, high, "gx", 1, 1).reshape(3, 3, 5, 3, B, 3 * B)
    part = fold(part[0], part[1], part[2], "gz", 4, B)
    part, targets = lax.optimization_barrier((part, targets))
    part = fold(part[0], part[1], part[2], "gy", 1, 1).astype(jnp.bfloat16)
    coarse = part.reshape(25, B, 5 * B).transpose(1, 0, 2).reshape(B, 125 * B)
    coarse = jnp.pad(coarse, ((0, 0), (0, 3 * B)))

    width = 128 * B // group_size
    spread = coarse.reshape(B, group_size, width).transpose(1, 0, 2)
    pieces = lax.all_to_all(spread, "gz", split_axis=0, concat_axis=0, tiled=True)
    group = lax.axis_index("gx") * lax.axis_size("gy") + lax.axis_index("gy")
    slots = group * (2 * group_size) + jnp.arange(2 * group_size, dtype=jnp.int32)
    matches = slots[:, None] == targets[None, :]
    source = jnp.argmax(matches, axis=1).astype(jnp.int32)
    taken = jnp.any(matches, axis=1)
    sent = jnp.take(pieces, source, axis=0, mode="clip")
    sent = jnp.where(taken[:, None, None], sent, jnp.zeros((), jnp.bfloat16))
    mine = lax.all_to_all(sent, "gz", split_axis=0, concat_axis=0, tiled=True)
    return mine.reshape(group_size, 2, B, width).transpose(1, 2, 0, 3).reshape(2, B, 128 * B)


def solution(mesh):
    in_specs = (
        P("gx", "gy", "gz", None, None),
        P("gx", "gy", "gz", None),
        P("gx", "gy", "gz"),
        P("gx", "gy", "gz", None, None),
        P("gx", "gy", "gz", None),
        P("gx", "gy", "gz"),
        P("gx", "gy", "gz"),
    )
    out_specs = P(("gx", "gy", "gz"), None, None)
    return jax.shard_map(local, mesh=mesh, in_specs=in_specs, out_specs=out_specs, check_vma=False)
```
